32 devices in a mesh: groups: 2 (over x), hist: 8 (over z, y), cand: 2 (over core).
Axes of the slice: x: 2, y: 2, z: 4, core: 2. Of those that a mesh axis runs over, the one named last changes fastest.
Arguments:
- candidates: bfloat16 [16, 1024, 512], P(('groups', 'hist'), 'cand'), parts along dimension 0, may hold values from -6 to 6
- hist_keys: bfloat16 [16, 1024, 512], P('groups', ('hist', 'cand')), parts along dimension 0, may hold values from -10 to 10
- hist_values: bfloat16 [16, 1024, 512], P('groups', ('hist', 'cand')), parts along dimension 0, may hold values from -6 to 6
- block_mask: int32 [16, 8, 8], P(('groups', 'hist')), parts along dimension 0, may hold values 0 or 1
- hist_blocks: int32 [16], P(('groups', 'hist')), parts along dimension 0, may hold values from 1 to 8, as said below
- proj_weight: bfloat16 [512, 1024], replicated, may hold values from -0.25 to 0.25
- out_weight: bfloat16 [512, 512], replicated, may hold values from -0.25 to 0.25
Outputs:
- cand_out: bfloat16 [16, 1024, 512], P(('groups', 'hist'), 'cand'), parts along dimension 0
The draws below stay inside these ranges and needn't reach their ends.
There are 2 independent parts, one for each index of `groups`. The reference program is written for one: setup_inputs(seed, part) draws one part's arguments, and reference() takes and returns one part's arrays. A program takes and returns all parts, laid end to end along the dimension named above; an argument that names none is the same for every part. Nothing has to cross between parts.
Inputs may be any that keep to these rules, and one draw needn't show every extreme that they name: `hist_blocks`: some user has all 8 blocks.
All inputs are finite; a program needn't handle non-finite values. No bound on the sum of `block_mask` on one device may be relied on, other than what follows from the above.
Results may differ from the reference program's by a relative error of at most 0.013.
Values may be sent and summed in bfloat16 or wider, within the bound.
A program may use at most 64 MiB of HBM per device.

```python
import jax
import jax.numpy as jnp
from jax import lax

D = 512
HEADS = 8
BLK = 128
USERS = 8
CANDS = 1024
HIST = 1024
HBLK = 8
CBLK = 8
DH = 64


def draw_hist_blocks(key, part):
    first_key, second_key = jax.random.split(jax.random.fold_in(key, 17))
    drawn = jax.random.randint(first_key, (USERS,), 1, HBLK + 1)
    chosen = jax.random.randint(second_key, (), 0, USERS)
    return jnp.where(jnp.arange(USERS) == chosen, HBLK, drawn).astype(jnp.int32)


def with_ends(values, own_key, low, high):
    dims = values.shape
    spot = [jax.random.randint(jax.random.fold_in(own_key, axis), (), 0, dims[axis]) for axis in range(len(dims))]
    values = values.at[tuple(spot)].set(low)
    longest = dims.index(max(dims))
    spot[longest] = (spot[longest] + 1) % dims[longest]
    return values.at[tuple(spot)].set(high)


def level_of(key, extent, cuts, low, largest):
    gain, own = 1.0, jax.random.fold_in(key, 6)
    for axis_at, parts in cuts:
        draws = jnp.exp(jax.random.uniform(jax.random.fold_in(own, axis_at), (parts,), jnp.float32, low / len(cuts), largest / len(cuts)))
        gain = gain * jnp.repeat(draws, extent[axis_at] // parts).reshape([-1 if axis == axis_at else 1 for axis in range(len(extent))])
    return gain


def gaussian(own_key, dims, width, most, pieces=(), dtype=jnp.bfloat16):
    values = jax.random.normal(own_key, dims, jnp.float32) * width
    if len(pieces) > 0:
        values = level_of(own_key, dims, pieces, -0.22, 0.18) * values
    return jnp.clip(values, min=-most, max=most).astype(dtype)


def setup_inputs(seed: int = 0, part: int = 0) -> dict:
    key_list = jax.random.split(jax.random.key(seed), 8)
    own_keys = jax.random.split(jax.random.fold_in(key_list[7], part), 8)
    candidates = gaussian(own_keys[0], (USERS, CANDS, D), 1.0, 6.0, ((0, 8), (1, 2)))
    hist_keys = gaussian(own_keys[1], (USERS, HIST, D), 2.0, 10.0, ((1, 16),))
    hist_values = gaussian(own_keys[2], (USERS, HIST, D), 1.0, 6.0, ((1, 16),))
    block_mask = with_ends((jax.random.randint(own_keys[3], (USERS, CBLK, HBLK), 0, 5) < 3).astype(jnp.int32), jax.random.fold_in(own_keys[3], 1), 0, 1)
    hist_blocks = draw_hist_blocks(jax.random.fold_in(jax.random.fold_in(key_list[7], part), 71), part)
    proj_weight = gaussian(key_list[5], (D, 2 * D), D ** -0.5, 0.25)
    out_weight = gaussian(key_list[6], (D, D), D ** -0.5, 0.25)
    return dict(candidates=candidates, hist_keys=hist_keys, hist_values=hist_values, block_mask=block_mask, hist_blocks=hist_blocks, proj_weight=proj_weight, out_weight=out_weight)


EPS = 1e-05

def layer_norm(values_in):
    center = values_in - lax.optimization_barrier(jnp.mean(values_in, axis=-1, keepdims=True))
    spread = lax.optimization_barrier(jnp.mean(center * center, axis=-1, keepdims=True))
    return center * lax.rsqrt(spread + EPS)

def one_user(cand_rows, key_rows, value_rows, mask_rows, length, proj_weight, out_weight):
    normed = layer_norm(cand_rows.astype(jnp.float32)).astype(jnp.bfloat16)
    projected = jax.nn.silu(jnp.dot(normed, proj_weight, preferred_element_type=jnp.float32)).astype(jnp.bfloat16)
    gate_rows = projected[:, :D]
    queries = projected[:, D:]
    live_blocks = (jnp.arange(HBLK) < length).astype(jnp.float32)
    mask_eff = mask_rows.astype(jnp.float32) * live_blocks[None, :]
    key_mask = jnp.repeat(jnp.repeat(mask_eff, BLK, axis=0), BLK, axis=1)
    query_heads = queries.reshape(CANDS, HEADS, DH).astype(jnp.float32)
    key_heads = key_rows.reshape(HIST, HEADS, DH).astype(jnp.float32)
    value_heads = value_rows.reshape(HIST, HEADS, DH).astype(jnp.float32)
    scores = jnp.einsum('chd,khd->hck', query_heads, key_heads) * DH ** (-0.5)
    weights = (jax.nn.silu(scores) * key_mask[None]).astype(jnp.bfloat16)
    attended = jnp.einsum('hck,khd->chd', weights.astype(jnp.float32), value_heads).reshape(CANDS, D)
    mixed = (layer_norm(attended) * gate_rows.astype(jnp.float32)).astype(jnp.bfloat16)
    result = cand_rows.astype(jnp.float32) + jnp.dot(mixed, out_weight, preferred_element_type=jnp.float32)
    return result.astype(jnp.bfloat16)

def reference(candidates, hist_keys, hist_values, block_mask, hist_blocks, proj_weight, out_weight):

    def per_user(packed):
        return one_user(packed[0], packed[1], packed[2], packed[3], packed[4], proj_weight, out_weight)
    return lax.map(per_user, (candidates, hist_keys, hist_values, block_mask, hist_blocks))
```

```python
import functools

import jax
import jax.numpy as jnp
from jax import lax
from jax.experimental import pallas as pl
from jax.experimental.pallas import tpu as pltpu
from jax.sharding import PartitionSpec as P

HEADS = 8
BLK = 128
GROUP = 4
EPS = 1e-05
MESH = pl.DeviceIdType.MESH


def layer_norm(values_in):
    center = values_in - jnp.mean(values_in, axis=-1, keepdims=True)
    spread = jnp.mean(center * center, axis=-1, keepdims=True)
    return center * lax.rsqrt(spread + EPS)


def silu(values_in):
    half = values_in * 0.5
    return half + half * jnp.tanh(half)


def partner_of(me, step, count):
    if count & (count - 1) == 0:
        other = 0
        bit = 1
        while bit < count:
            other = other + ((me // bit + step // bit) % 2) * bit
            bit *= 2
        return other, other
    return (me + count - step) % count, (me + step) % count


def spread_heads(piece, head_size):
    width = piece.shape[1]
    lanes = lax.broadcasted_iota(jnp.int32, piece.shape, 1) // head_size
    zero = jnp.zeros_like(piece)
    return jnp.concatenate(
        [jnp.where(lanes == head, piece, zero) for head in range(width // head_size)], axis=0
    )


def kernel(
    hist_count, cand_count,
    mask_ref, len_ref, cand_hbm, keys_hbm, values_hbm, proj_hbm, outw_hbm,
    out_ref,
    cand_v, proj_v, outw_v, key_buf, value_buf, query_v, gate_v, total_v, masked_v,
    in_sem, own_sem, send_sem, recv_sem, fsend_sem, frecv_sem,
):
    me = lax.axis_index("hist")
    core = lax.axis_index("cand")
    own_rows, width = cand_v.shape
    head_size = width // HEADS
    group_width = GROUP * head_size
    own_blocks = own_rows // BLK
    scale = 0.5 * head_size ** (-0.5)

    cand_in = pltpu.make_async_copy(cand_hbm.at[0], cand_v, in_sem.at[0])
    proj_in = pltpu.make_async_copy(proj_hbm, proj_v, in_sem.at[1])
    outw_in = pltpu.make_async_copy(outw_hbm, outw_v, in_sem.at[2])
    cand_in.start()
    proj_in.start()
    outw_in.start()
    own_in = [
        pltpu.make_async_copy(src.at[me], buf.at[0, core], own_sem.at[i])
        for i, (src, buf) in enumerate(((keys_hbm, key_buf), (values_hbm, value_buf)))
    ]
    for copy in own_in:
        copy.start()

    barrier = pltpu.get_barrier_semaphore()
    for step in range(1, hist_count):
        _, dst = partner_of(me, step, hist_count)
        pl.semaphore_signal(barrier, inc=1, device_id={"hist": dst}, device_id_type=MESH)
    for turn in range(1, cand_count):
        pl.semaphore_signal(
            barrier, inc=1, device_id={"cand": (core + turn) % cand_count}, device_id_type=MESH
        )
    pl.semaphore_wait(barrier, hist_count - 1 + cand_count - 1)

    def direct(step, kind):
        _, dst = partner_of(me, step, hist_count)
        src, buf = ((keys_hbm, key_buf), (values_hbm, value_buf))[kind]
        return pltpu.make_async_remote_copy(
            src_ref=src.at[dst],
            dst_ref=buf.at[step, core],
            send_sem=send_sem.at[step, kind],
            recv_sem=recv_sem.at[step, kind],
            device_id={"hist": dst},
            device_id_type=MESH,
        )

    def forward(step, kind, turn, first=False):
        src, buf = ((keys_hbm, key_buf), (values_hbm, value_buf))[kind]
        return pltpu.make_async_remote_copy(
            src_ref=src.at[me] if first else buf.at[step, core],
            dst_ref=buf.at[step, core],
            send_sem=fsend_sem.at[step, turn - 1, kind],
            recv_sem=frecv_sem.at[step, turn - 1, kind],
            device_id={"cand": (core + turn) % cand_count},
            device_id_type=MESH,
        )

    for step in range(1, hist_count):
        for kind in range(2):
            direct(step, kind).start()
    for turn in range(1, cand_count):
        for kind in range(2):
            forward(0, kind, turn, True).start()

    cand_in.wait()
    proj_in.wait()
    normed = layer_norm(cand_v[...].astype(jnp.float32)).astype(jnp.bfloat16)
    gate_v[...] = silu(
        jnp.dot(normed, proj_v[:, :width], preferred_element_type=jnp.float32)
    ).astype(jnp.bfloat16)
    query_v[...] = silu(
        jnp.dot(normed, proj_v[:, width:], preferred_element_type=jnp.float32)
    ).astype(jnp.bfloat16)
    total_v[...] = jnp.zeros_like(total_v)

    def mask_queries(step):
        source, _ = partner_of(me, step, hist_count)
        live = jnp.clip(len_ref[0] - source, 0, 1)
        for block in range(own_blocks):
            factor = (mask_ref[0, core * own_blocks + block, source] * live).astype(
                jnp.float32
            ) * scale
            rows = pl.ds(block * BLK, BLK)
            masked_v[rows, :] = (query_v[rows, :].astype(jnp.float32) * factor).astype(jnp.bfloat16)

    def attend(step, owner):
        for group in range(width // group_width):
            columns = pl.ds(group * group_width, group_width)
            keys = spread_heads(key_buf[step, owner, :, columns], head_size)
            values = spread_heads(value_buf[step, owner, :, columns], head_size)
            half = lax.dot_general(
                masked_v[:, columns], keys, (((1,), (1,)), ((), ())),
                preferred_element_type=jnp.float32,
            )
            weights = (half + half * jnp.tanh(half)).astype(jnp.bfloat16)
            total_v[:, columns] += jnp.dot(weights, values, preferred_element_type=jnp.float32)

    def others(step):
        for turn in range(1, cand_count):
            for kind in range(2):
                forward(step, kind, turn).wait_recv()
            attend(step, (core + cand_count - turn) % cand_count)

    mask_queries(0)
    for copy in own_in:
        copy.wait()
    attend(0, core)
    others(0)

    def one_step(step, carry):
        mask_queries(step)
        for kind in range(2):
            direct(step, kind).wait_recv()
            for turn in range(1, cand_count):
                forward(step, kind, turn).start()
        attend(step, core)
        others(step)
        return carry

    lax.fori_loop(1, hist_count, one_step, 0)

    outw_in.wait()
    mixed = (layer_norm(total_v[...]) * gate_v[...].astype(jnp.float32)).astype(jnp.bfloat16)
    result = cand_v[...].astype(jnp.float32) + jnp.dot(
        mixed, outw_v[...], preferred_element_type=jnp.float32
    )
    out_ref[0] = result.astype(jnp.bfloat16)

    for turn in range(1, cand_count):
        for kind in range(2):
            forward(0, kind, turn, True).wait_send()

    def drain(step, carry):
        for kind in range(2):
            direct(step, kind).wait_send()
            for turn in range(1, cand_count):
                forward(step, kind, turn).wait_send()
        return carry

    lax.fori_loop(1, hist_count, drain, 0)


def on_device(candidates, hist_keys, hist_values, block_mask, hist_blocks, proj_weight, out_weight):
    hist_count = lax.axis_size("hist")
    cand_count = lax.axis_size("cand")
    _, own_rows, width = candidates.shape
    piece = hist_keys.shape[1]
    anywhere = pl.BlockSpec(memory_space=pl.ANY)
    scalars = pl.BlockSpec(memory_space=pltpu.SMEM)
    bf16 = jnp.bfloat16
    return pl.pallas_call(
        functools.partial(kernel, hist_count, cand_count),
        out_shape=jax.ShapeDtypeStruct(candidates.shape, bf16),
        in_specs=[scalars, scalars] + [anywhere] * 5,
        out_specs=pl.BlockSpec(memory_space=pltpu.VMEM),
        scratch_shapes=[
            pltpu.VMEM((own_rows, width), bf16),
            pltpu.VMEM(proj_weight.shape, bf16),
            pltpu.VMEM(out_weight.shape, bf16),
            pltpu.VMEM((hist_count, cand_count, piece, width), bf16),
            pltpu.VMEM((hist_count, cand_count, piece, width), bf16),
            pltpu.VMEM((own_rows, width), bf16),
            pltpu.VMEM((own_rows, width), bf16),
            pltpu.VMEM((own_rows, width), jnp.float32),
            pltpu.VMEM((own_rows, width), bf16),
            pltpu.SemaphoreType.DMA((3,)),
            pltpu.SemaphoreType.DMA((2,)),
            pltpu.SemaphoreType.DMA((hist_count, 2)),
            pltpu.SemaphoreType.DMA((hist_count, 2)),
            pltpu.SemaphoreType.DMA((hist_count, max(cand_count - 1, 1), 2)),
            pltpu.SemaphoreType.DMA((hist_count, max(cand_count - 1, 1), 2)),
        ],
        compiler_params=pltpu.CompilerParams(collective_id=0, has_side_effects=True),
    )(block_mask, hist_blocks, candidates, hist_keys, hist_values, proj_weight, out_weight)


def solution(mesh):
    in_specs = (
        P(("groups", "hist"), "cand", None),
        P("groups", ("hist", "cand"), None),
        P("groups", ("hist", "cand"), None),
        P(("groups", "hist"), None, None),
        P(("groups", "hist")),
        P(),
        P(),
    )
    out_specs = P(("groups", "hist"), "cand", None)
    return jax.shard_map(
        on_device, mesh=mesh, in_specs=in_specs, out_specs=out_specs, check_vma=False
    )
```

```python
import functools

import jax
import jax.numpy as jnp
from jax import lax
from jax.experimental import pallas as pl
from jax.experimental.pallas import tpu as pltpu
from jax.sharding import PartitionSpec as P

HEADS = 8
BLK = 128
GROUP = 4
UNROLLED = 8
EPS = 1e-05
MESH = pl.DeviceIdType.MESH


def layer_norm(values_in):
    center = values_in - jnp.mean(values_in, axis=-1, keepdims=True)
    spread = jnp.mean(center * center, axis=-1, keepdims=True)
    return center * lax.rsqrt(spread + EPS)


def silu(values_in):
    half = values_in * 0.5
    return half + half * jnp.tanh(half)


def partner_of(me, step, count):
    if count & (count - 1) == 0:
        other = 0
        bit = 1
        while bit < count:
            other = other + ((me // bit + step // bit) % 2) * bit
            bit *= 2
        return other, other
    return (me + count - step) % count, (me + step) % count


def step_order(count):
    if count & (count - 1) or count < 4:
        return list(range(1, count))
    bits = (count // 2).bit_length() - 1
    order = []
    for pair in range(count // 2):
        turned = sum((pair >> bit & 1) << (bits - 1 - bit) for bit in range(bits))
        order += [turned * 2, turned * 2 + 1]
    return order[1:]


def spread_heads(piece, head_size):
    width = piece.shape[1]
    lanes = lax.broadcasted_iota(jnp.int32, piece.shape, 1) // head_size
    zero = jnp.zeros_like(piece)
    return jnp.concatenate(
        [jnp.where(lanes == head, piece, zero) for head in range(width // head_size)], axis=0
    )


def kernel(
    hist_count, cand_count,
    mask_ref, len_ref, cand_hbm, keys_hbm, values_hbm, proj_hbm, outw_hbm,
    out_ref,
    cand_v, proj_v, outw_v, key_buf, value_buf, query_v, gate_v, total_v, masked_v,
    in_sem, own_sem, send_sem, recv_sem, fsend_sem, frecv_sem,
):
    me = lax.axis_index("hist")
    core = lax.axis_index("cand")
    own_rows, width = cand_v.shape
    head_size = width // HEADS
    group_width = GROUP * head_size
    own_blocks = own_rows // BLK
    scale = 0.5 * head_size ** (-0.5)

    cand_in = pltpu.make_async_copy(cand_hbm.at[0], cand_v, in_sem.at[0])
    proj_in = pltpu.make_async_copy(proj_hbm, proj_v, in_sem.at[1])
    outw_in = pltpu.make_async_copy(outw_hbm, outw_v, in_sem.at[2])
    cand_in.start()
    proj_in.start()
    outw_in.start()
    own_in = [
        pltpu.make_async_copy(src.at[me], buf.at[0, core], own_sem.at[i])
        for i, (src, buf) in enumerate(((keys_hbm, key_buf), (values_hbm, value_buf)))
    ]
    for copy in own_in:
        copy.start()

    barrier = pltpu.get_barrier_semaphore()
    for step in range(1, hist_count):
        _, dst = partner_of(me, step, hist_count)
        pl.semaphore_signal(barrier, inc=1, device_id={"hist": dst}, device_id_type=MESH)
    for turn in range(1, cand_count):
        pl.semaphore_signal(
            barrier, inc=1, device_id={"cand": (core + turn) % cand_count}, device_id_type=MESH
        )
    pl.semaphore_wait(barrier, hist_count - 1 + cand_count - 1)

    def direct(step, kind):
        _, dst = partner_of(me, step, hist_count)
        src, buf = ((keys_hbm, key_buf), (values_hbm, value_buf))[kind]
        return pltpu.make_async_remote_copy(
            src_ref=src.at[dst],
            dst_ref=buf.at[step, core],
            send_sem=send_sem.at[step, kind],
            recv_sem=recv_sem.at[step, kind],
            device_id={"hist": dst},
            device_id_type=MESH,
        )

    def forward(step, kind, turn, first=False):
        src, buf = ((keys_hbm, key_buf), (values_hbm, value_buf))[kind]
        return pltpu.make_async_remote_copy(
            src_ref=src.at[me] if first else buf.at[step, core],
            dst_ref=buf.at[step, core],
            send_sem=fsend_sem.at[step, turn - 1, kind],
            recv_sem=frecv_sem.at[step, turn - 1, kind],
            device_id={"cand": (core + turn) % cand_count},
            device_id_type=MESH,
        )

    order = step_order(hist_count)
    for step in order:
        for kind in range(2):
            direct(step, kind).start()
    for turn in range(1, cand_count):
        for kind in range(2):
            forward(0, kind, turn, True).start()

    cand_in.wait()
    proj_in.wait()
    normed = layer_norm(cand_v[...].astype(jnp.float32)).astype(jnp.bfloat16)
    gate_v[...] = silu(
        jnp.dot(normed, proj_v[:, :width], preferred_element_type=jnp.float32)
    ).astype(jnp.bfloat16)
    query_v[...] = silu(
        jnp.dot(normed, proj_v[:, width:], preferred_element_type=jnp.float32)
    ).astype(jnp.bfloat16)
    total_v[...] = jnp.zeros_like(total_v)

    def mask_queries(step):
        source, _ = partner_of(me, step, hist_count)
        live = jnp.clip(len_ref[0] - source, 0, 1)
        for block in range(own_blocks):
            factor = (mask_ref[0, core * own_blocks + block, source] * live).astype(
                jnp.float32
            ) * scale
            rows = pl.ds(block * BLK, BLK)
            masked_v[rows, :] = (query_v[rows, :].astype(jnp.float32) * factor).astype(jnp.bfloat16)

    def attend(step, owner):
        for group in range(width // group_width):
            columns = pl.ds(group * group_width, group_width)
            keys = spread_heads(key_buf[step, owner, :, columns], head_size)
            values = spread_heads(value_buf[step, owner, :, columns], head_size)
            half = lax.dot_general(
                masked_v[:, columns], keys, (((1,), (1,)), ((), ())),
                preferred_element_type=jnp.float32,
            )
            weights = (half + half * jnp.tanh(half)).astype(jnp.bfloat16)
            total_v[:, columns] += jnp.dot(weights, values, preferred_element_type=jnp.float32)

    def others(step):
        for turn in range(1, cand_count):
            for kind in range(2):
                forward(step, kind, turn).wait_recv()
            attend(step, (core + cand_count - turn) % cand_count)

    mask_queries(0)
    for copy in own_in:
        copy.wait()
    attend(0, core)
    others(0)

    def one_step(step, carry):
        mask_queries(step)
        for kind in range(2):
            direct(step, kind).wait_recv()
            for turn in range(1, cand_count):
                forward(step, kind, turn).start()
        attend(step, core)
        others(step)
        return carry

    if hist_count <= UNROLLED:
        for step in order:
            one_step(step, 0)
    else:
        lax.fori_loop(1, hist_count, one_step, 0)

    outw_in.wait()
    mixed = (layer_norm(total_v[...]) * gate_v[...].astype(jnp.float32)).astype(jnp.bfloat16)
    result = cand_v[...].astype(jnp.float32) + jnp.dot(
        mixed, outw_v[...], preferred_element_type=jnp.float32
    )
    out_ref[0] = result.astype(jnp.bfloat16)

    for turn in range(1, cand_count):
        for kind in range(2):
            forward(0, kind, turn, True).wait_send()

    def drain(step, carry):
        for kind in range(2):
            direct(step, kind).wait_send()
            for turn in range(1, cand_count):
                forward(step, kind, turn).wait_send()
        return carry

    lax.fori_loop(1, hist_count, drain, 0)


def on_device(candidates, hist_keys, hist_values, block_mask, hist_blocks, proj_weight, out_weight):
    hist_count = lax.axis_size("hist")
    cand_count = lax.axis_size("cand")
    _, own_rows, width = candidates.shape
    piece = hist_keys.shape[1]
    anywhere = pl.BlockSpec(memory_space=pl.ANY)
    scalars = pl.BlockSpec(memory_space=pltpu.SMEM)
    bf16 = jnp.bfloat16
    return pl.pallas_call(
        functools.partial(kernel, hist_count, cand_count),
        out_shape=pltpu.VMEM(candidates.shape, bf16),
        in_specs=[scalars, scalars] + [anywhere] * 5,
        out_specs=pl.BlockSpec(memory_space=pltpu.VMEM),
        scratch_shapes=[
            pltpu.VMEM((own_rows, width), bf16),
            pltpu.VMEM(proj_weight.shape, bf16),
            pltpu.VMEM(out_weight.shape, bf16),
            pltpu.VMEM((hist_count, cand_count, piece, width), bf16),
            pltpu.VMEM((hist_count, cand_count, piece, width), bf16),
            pltpu.VMEM((own_rows, width), bf16),
            pltpu.VMEM((own_rows, width), bf16),
            pltpu.VMEM((own_rows, width), jnp.float32),
            pltpu.VMEM((own_rows, width), bf16),
            pltpu.SemaphoreType.DMA((3,)),
            pltpu.SemaphoreType.DMA((2,)),
            pltpu.SemaphoreType.DMA((hist_count, 2)),
            pltpu.SemaphoreType.DMA((hist_count, 2)),
            pltpu.SemaphoreType.DMA((hist_count, max(cand_count - 1, 1), 2)),
            pltpu.SemaphoreType.DMA((hist_count, max(cand_count - 1, 1), 2)),
        ],
        compiler_params=pltpu.CompilerParams(collective_id=0, has_side_effects=True),
    )(block_mask, hist_blocks, candidates, hist_keys, hist_values, proj_weight, out_weight)


def solution(mesh):
    in_specs = (
        P(("groups", "hist"), "cand", None),
        P("groups", ("hist", "cand"), None),
        P("groups", ("hist", "cand"), None),
        P(("groups", "hist"), None, None),
        P(("groups", "hist")),
        P(),
        P(),
    )
    out_specs = P(("groups", "hist"), "cand", None)
    return jax.shard_map(
        on_device, mesh=mesh, in_specs=in_specs, out_specs=out_specs, check_vma=False
    )
```
